256 devices in a mesh: row: 32 (over x, z_hi, core), col: 8 (over z_lo, y).
Axes of the slice: x: 4, y: 4, z: 8 (z_hi: 4, z_lo: 2; z = z_hi * 2 + z_lo), core: 2. Of those that a mesh axis runs over, the one named last changes fastest.
Arguments:
- inputs: bfloat16 [16384, 5376], P('row', 'col'), may hold values from -6 to 6
- norm_gain: float32 [5376], replicated, may hold values from 0.1 to 1.9
- w_query: bfloat16 [5376, 4096], P('row', 'col'), may hold values from -1 to 1
- w_key: bfloat16 [5376, 2048], P('row', 'col'), may hold values from -2 to 2
- w_value: bfloat16 [5376, 2048], P('row', 'col'), may hold values from -0.078125 to 0.078125
- w_out: bfloat16 [4096, 5376], P('col', 'row'), may hold values from -0.09375 to 0.09375
- q_gain: float32 [128], replicated, may hold values from 0.5 to 5
- k_gain: float32 [128], replicated, may hold values from 0.5 to 5
Outputs:
- attended: bfloat16 [16384, 5376], P('row', 'col')
The draws below stay inside these ranges and needn't reach their ends.
All inputs are finite; a program needn't handle non-finite values.
Results may differ from the reference program's by a relative error of at most 0.017.
Values may be sent and summed in bfloat16 or wider, within the bound.
No kernel may reach another device: no remote copies, remote signals or barrier semaphores. Data moves between devices by JAX's collectives and lax.ppermute only.
A program may use at most 64 MiB of HBM per device.

```python
import jax
import jax.numpy as jnp
from jax import lax

D = 5376
HEADS = 32
KVH = 16
HD = 128
WIN = 1024
TOK_DEV = 512
TOKENS = 16384
QW = 4096
KW = 2048
N_ROW = 32
N_COL = 8


def draw_shared(key):
    return jax.random.truncated_normal(jax.random.fold_in(key, 11), -6.0, 6.0, (D, HEADS * HD), jnp.float32)


def draw_w_query(key, part):
    return (draw_shared(key) * D ** (-0.5)).astype(jnp.bfloat16)


def draw_w_key(key, part):
    noise = jax.random.truncated_normal(jax.random.fold_in(key, 12), -6.0, 6.0, (D, KVH * HD), jnp.float32)
    mixed = noise
    return (mixed * D ** (-0.5)).astype(jnp.bfloat16)


def draw_q_gain(key, part):
    inner = jax.random.fold_in(key, 21)
    return jax.random.uniform(inner, (HD,), jnp.float32, 0.6, 1.6)


def draw_k_gain(key, part):
    inner = jax.random.fold_in(key, 22)
    return jax.random.uniform(inner, (HD,), jnp.float32, 0.6, 1.6)


def levels(key, shape, split, low, high):
    loudness = 1.0
    for position, blocks in split:
        heights = jax.random.uniform(jax.random.fold_in(jax.random.fold_in(key, 6), position), (blocks,), jnp.float32, low / len(split), high / len(split))
        loudness = loudness * jnp.repeat(jnp.exp(heights), shape[position] // blocks).reshape((-1,) + (1,) * (len(shape) - 1 - position))
    return loudness


def bell_draw(stream_key, shape, width, reach, pieces=(), kind=jnp.bfloat16):
    array = width * jax.random.normal(stream_key, shape, jnp.float32)
    if pieces:
        array = array * levels(stream_key, shape, pieces, -0.22, 0.18)
    return jnp.clip(array, -reach, reach).astype(kind)


def setup_inputs(seed: int = 0) -> dict:
    key_of = jax.random.split(jax.random.key(seed), 9)
    return {
        "inputs": bell_draw(key_of[0], (TOKENS, D), 1.0, 6.0, ((0, 32), (1, 8))),
        "norm_gain": jnp.clip(1.0 + 0.18 * jax.random.normal(key_of[1], (D,), jnp.float32), 0.1, 1.9),
        "w_query": draw_w_query(jax.random.fold_in(key_of[8], 71), 0),
        "w_key": draw_w_key(jax.random.fold_in(key_of[8], 71), 0),
        "w_value": bell_draw(key_of[4], (D, KW), D ** -0.5, 0.078125, ((0, 32), (1, 8))),
        "w_out": bell_draw(key_of[5], (QW, D), QW ** -0.5, 0.09375, ((0, 8), (1, 32))),
        "q_gain": draw_q_gain(jax.random.fold_in(key_of[8], 71), 0),
        "k_gain": draw_k_gain(jax.random.fold_in(key_of[8], 71), 0),
    }


epsilon = 1e-06
score_scale = 168.0 ** (-0.5)

def rotate_pairs(values, positions):
    half_dim = values.shape[-1] // 2
    frequency = jnp.exp(-(jnp.arange(half_dim, dtype=jnp.float32) * (2.0 / values.shape[-1])) * jnp.log(jnp.float32(10000.0)))
    angles = positions[:, None] * frequency[None, :]
    cosine = jnp.cos(angles)[:, None, :]
    sine = jnp.sin(angles)[:, None, :]
    first = values[..., :half_dim]
    second = values[..., half_dim:]
    return jnp.concatenate([first * cosine - second * sine, second * cosine + first * sine], axis=-1)

def head_rms(values, gain):
    return values * lax.rsqrt(lax.optimization_barrier(jnp.mean(values * values, axis=-1, keepdims=True)) + epsilon) * gain

def reference(inputs, norm_gain, w_query, w_key, w_value, w_out, q_gain, k_gain):
    input_float = inputs.astype(jnp.float32)
    mean_sq = lax.optimization_barrier(jnp.mean(input_float * input_float, axis=1, keepdims=True))
    normed = (input_float * lax.rsqrt(mean_sq + epsilon) * norm_gain).astype(jnp.bfloat16)
    query_proj = jnp.dot(normed, w_query, preferred_element_type=jnp.float32).reshape(TOKENS, HEADS, HD)
    key_proj = jnp.dot(normed, w_key, preferred_element_type=jnp.float32).reshape(TOKENS, KVH, HD)
    value_proj = jnp.dot(normed, w_value, preferred_element_type=jnp.float32).reshape(TOKENS, KVH, HD)
    positions = jnp.arange(TOKENS, dtype=jnp.int32).astype(jnp.float32)
    query_rot = rotate_pairs(head_rms(query_proj, q_gain), positions).astype(jnp.bfloat16)
    key_rot = rotate_pairs(head_rms(key_proj, k_gain), positions).astype(jnp.bfloat16)
    value_rows = value_proj.astype(jnp.bfloat16)
    behind = (WIN - 2) // TOK_DEV + 1
    padding = behind * TOK_DEV
    key_padded = jnp.concatenate([jnp.zeros((padding, KVH, HD), jnp.bfloat16), key_rot], axis=0)
    value_padded = jnp.concatenate([jnp.zeros((padding, KVH, HD), jnp.bfloat16), value_rows], axis=0)

    def attend_block(index):
        start = (index * TOK_DEV).astype(jnp.int32)
        query_block = lax.dynamic_slice_in_dim(query_rot, start, TOK_DEV, 0).reshape(TOK_DEV, KVH, 2, HD)
        key_block = lax.dynamic_slice_in_dim(key_padded, start, padding + TOK_DEV, 0)
        value_block = lax.dynamic_slice_in_dim(value_padded, start, padding + TOK_DEV, 0)
        query_pos = start + jnp.arange(TOK_DEV, dtype=jnp.int32)
        key_pos = start - padding + jnp.arange(padding + TOK_DEV, dtype=jnp.int32)
        scores = jnp.einsum('qhgd,khd->hgqk', query_block.astype(jnp.float32), key_block.astype(jnp.float32)) * score_scale
        allowed = (key_pos[None, :] <= query_pos[:, None]) & (query_pos[:, None] - key_pos[None, :] < WIN) & (key_pos[None, :] >= 0)
        scores = jnp.where(allowed, scores, -1e+30)
        highest = lax.optimization_barrier(jnp.max(scores, axis=-1, keepdims=True))
        weights = jnp.exp(scores - highest)
        probs = (weights / lax.optimization_barrier(jnp.sum(weights, axis=-1, keepdims=True))).astype(jnp.bfloat16)
        heads_out = jnp.einsum('hgqk,khd->qhgd', probs.astype(jnp.float32), value_block.astype(jnp.float32))
        return heads_out.astype(jnp.bfloat16).reshape(TOK_DEV, QW)
    heads_out = lax.map(attend_block, jnp.arange(N_ROW, dtype=jnp.int32)).reshape(TOKENS, QW)
    group_width = QW // N_COL
    summed = jnp.zeros((TOKENS, D), jnp.float32)
    for group in range(N_COL):
        partial_value = jnp.dot(heads_out[:, group * group_width:(group + 1) * group_width], w_out[group * group_width:(group + 1) * group_width], preferred_element_type=jnp.float32)
        summed = summed + partial_value.astype(jnp.bfloat16).astype(jnp.float32)
    return summed.astype(jnp.bfloat16)
```

```python
import jax
import jax.numpy as jnp
from jax import lax
from jax.sharding import PartitionSpec as P

HD = 128
WIN = 1024
BF = jnp.bfloat16
F32 = jnp.float32


epsilon = 1e-06
score_scale = 168.0 ** (-0.5)

NX, NZ, NC, NZL, NY = 4, 4, 2, 2, 4


def row_perm(v, dx=0, dz=0, dc=0):
    route = []
    for x in range(NX):
        for z in range(NZ):
            for c in range(NC):
                to = ((x + dx) % NX * NZ + (z + dz) % NZ) * NC + (c + dc) % NC
                route.append(((x * NZ + z) * NC + c, to))
    return lax.ppermute(v, "row", route)


def col_perm(v, dz=0, dy=0):
    route = []
    for z in range(NZL):
        for y in range(NY):
            route.append((z * NY + y, (z + dz) % NZL * NY + (y + dy) % NY))
    return lax.ppermute(v, "col", route)


def fence(*values):
    return lax.optimization_barrier(values)


def angles(rows, first_pos):
    half = HD // 2
    frequency = jnp.exp(
        -(jnp.arange(half, dtype=F32) * (2.0 / HD)) * jnp.log(F32(10000.0))
    )
    positions = (first_pos + jnp.arange(rows, dtype=jnp.int32)).astype(F32)
    turn = frequency[:, None] * positions[None, :]
    return jnp.cos(turn), jnp.sin(turn)


def norm_rope(values, gain, cosine, sine):
    mean_sq = jnp.mean(values * values, axis=1, keepdims=True)
    scaled = values * lax.rsqrt(mean_sq + epsilon) * gain[None, :, None]
    first, second = scaled[:, : HD // 2], scaled[:, HD // 2 :]
    return jnp.concatenate(
        [first * cosine - second * sine, second * cosine + first * sine], axis=1
    ).astype(BF)


def shards(inputs, norm_gain, w_query, w_key, w_value, w_out, q_gain, k_gain):
    tokens, width = inputs.shape
    rows = w_query.shape[0]
    q_w, kv_w = w_query.shape[1], w_key.shape[1]
    heads, kv_heads = q_w // HD, kv_w // HD
    n_row, n_col = NX * NZ * NC, NZL * NY
    r, c = lax.axis_index("row"), lax.axis_index("col")
    xi, zi, k = r // (NZ * NC), r // NC % NZ, r % NC
    zl, y = c // NY, c % NY

    x = inputs.T
    w = jnp.concatenate([w_query, w_key, w_value], axis=1)
    o = w_out.T
    wh, xh = rows // 2 // 8 * 8, width // 2 // 8 * 8

    za, zb = row_perm(w, dz=1), row_perm(w, dz=-1)
    xa, xb = row_perm(w, dx=1), row_perm(w, dx=-1)
    ya, yb = col_perm(x, dy=1), col_perm(x, dy=-1)
    w, x, o, za, zb, xa, xb, ya, yb = fence(w, x, o, za, zb, xa, xb, ya, yb)
    p = col_perm(x, dz=1)
    z2a, z2b = row_perm(za[:wh], dz=1), row_perm(zb[wh:], dz=-1)
    yfa, yfb = col_perm(ya[:xh], dy=1), col_perm(yb[xh:], dy=-1)
    zz = jnp.stack([za, zb])
    xza, xzb = row_perm(zz, dx=1), row_perm(zz, dx=-1)
    xfa, xfb = row_perm(xa[:wh], dx=1), row_perm(xb[wh:], dx=-1)
    (p, z2a, z2b, yfa, yfb, xza, xzb, xfa, xfb, za, zb, xa, xb, o) = fence(
        p, z2a, z2b, yfa, yfb, xza, xzb, xfa, xfb, za, zb, xa, xb, o
    )
    pya, pyb = col_perm(p, dy=1), col_perm(p, dy=-1)
    z2 = jnp.concatenate([z2a, z2b], 0)
    xz2a, xz2b = row_perm(z2, dx=1), row_perm(z2, dx=-1)
    xzfa, xzfb = row_perm(xza[:, :wh], dx=1), row_perm(xzb[:, wh:], dx=-1)
    own = jnp.stack([w, za, zb, xa, xb])
    cown = row_perm(own, dc=1)
    oza, ozb = row_perm(o, dz=1), row_perm(o, dz=-1)
    (pya, pyb, xz2a, xz2b, xzfa, xzfb, z2, xza, xzb, xfa, xfb, oza, ozb) = fence(
        pya, pyb, xz2a, xz2b, xzfa, xzfb, z2, xza, xzb, xfa, xfb, oza, ozb
    )
    pfa, pfb = col_perm(pya[:xh], dy=1), col_perm(pyb[xh:], dy=-1)
    x2fa, x2fb = row_perm(xz2a[:wh], dx=1), row_perm(xz2b[wh:], dx=-1)
    x2ga = row_perm(xz2a[:wh], dx=1, dc=1)
    x2gb = row_perm(xz2b[wh:], dx=-1, dc=1)
    oz2a, oz2b = row_perm(oza[:wh], dz=1), row_perm(ozb[wh:], dz=-1)
    xf = jnp.concatenate([xfa, xfb], 0)
    xzf = jnp.concatenate([xzfa, xzfb], 1)
    sec = jnp.concatenate([xza, xzb, xzf, jnp.stack([z2, xz2a, xz2b, xf])], 0)
    csec = row_perm(sec, dc=1)
    (pfa, pfb, x2fa, x2fb, x2ga, x2gb, sec, csec, oz2a, oz2b, oza, ozb, o) = fence(
        pfa, pfb, x2fa, x2fb, x2ga, x2gb, sec, csec, oz2a, oz2b, oza, ozb, o
    )

    weights = jnp.zeros((n_row, rows, w.shape[1]), BF)

    def put(block, dx, dz, dc):
        at = ((xi + dx) % NX * NZ + (zi + dz) % NZ) * NC + (k + dc) % NC
        return lax.dynamic_update_slice(weights, block[None], (at, 0, 0))

    near = [(0, 0), (0, -1), (0, 1), (-1, 0), (1, 0)]
    far = [(-1, -1), (-1, 1), (1, -1), (1, 1), (2, -1), (2, 1)]
    far = far + [(0, 2), (-1, 2), (1, 2), (2, 0)]
    last = jnp.concatenate([x2fa, x2fb], 0), jnp.concatenate([x2ga, x2gb], 0)
    for dc, first, second in ((0, own, sec), (1, cown, csec)):
        for j, (dx, dz) in enumerate(near):
            weights = put(first[j], dx, dz, dc)
        for j, (dx, dz) in enumerate(far):
            weights = put(second[j], dx, dz, dc)
        weights = put(last[dc], 2, 2, dc)
    weights = weights.reshape(n_row * rows, -1)

    full = jnp.zeros((n_col, width, tokens), BF)
    yf, pf = jnp.concatenate([yfa, yfb], 0), jnp.concatenate([pfa, pfb], 0)
    for block, dz, dy in [
        (x, 0, 0), (ya, 0, -1), (yb, 0, 1), (yf, 0, 2),
        (p, 1, 0), (pya, 1, -1), (pyb, 1, 1), (pf, 1, 2),
    ]:
        at = (zl + dz) % NZL * NY + (y + dy) % NY
        full = lax.dynamic_update_slice(full, block[None], (at, 0, 0))
    full = full.reshape(n_col * width, tokens)

    floats = full.astype(F32)
    mean_sq = jnp.mean(floats * floats, axis=0, keepdims=True)
    normed = (floats * lax.rsqrt(mean_sq + epsilon) * norm_gain[:, None]).astype(BF)
    proj = lax.dot_general(
        weights, normed, (((0,), (0,)), ((), ())), preferred_element_type=F32
    )

    oz2 = jnp.concatenate([oz2a, oz2b], 0)
    ozs = jnp.zeros((NZ, rows, o.shape[1]), BF)
    for block, dz in ((o, 0), (oza, -1), (ozb, 1), (oz2, 2)):
        ozs = lax.dynamic_update_slice(ozs, block[None], ((zi + dz) % NZ, 0, 0))
    oxa, oxb = row_perm(ozs, dx=1), row_perm(ozs, dx=-1)

    first_pos = r * tokens
    cosine, sine = angles(tokens, first_pos)
    query = norm_rope(proj[:q_w].reshape(heads, HD, tokens), q_gain, cosine, sine)
    key = norm_rope(
        proj[q_w : q_w + kv_w].reshape(kv_heads, HD, tokens), k_gain, cosine, sine
    )
    value = proj[q_w + kv_w :].reshape(kv_heads, HD, tokens).astype(BF)
    kv = jnp.stack([key, value])
    query, kv, oxa, oxb, ozs = fence(query, kv, oxa, oxb, ozs)
    behind2 = lax.ppermute(kv, "row", [(i, i + 2) for i in range(n_row - 2)])
    mate = lax.ppermute(kv, "row", [(i, i + 1) for i in range(0, n_row, 2)])
    oxfa, oxfb = row_perm(oxa[:2], dx=1), row_perm(oxb[2:], dx=-1)
    kv, behind2, mate, oxfa, oxfb = fence(kv, behind2, mate, oxfa, oxfb)
    passed = lax.ppermute(behind2, "row", [(i + 1, i) for i in range(0, n_row, 2)])
    oxf = jnp.concatenate([oxfa, oxfb], 0)
    oall = jnp.zeros((NX,) + ozs.shape, BF)
    for block, dx in ((ozs, 0), (oxa, -1), (oxb, 1), (oxf, 2)):
        oall = lax.dynamic_update_slice(oall, block[None], ((xi + dx) % NX, 0, 0, 0))
    ocore = row_perm(oall, dc=1)
    behind1 = jnp.where(k == 0, passed, mate)
    window = jnp.concatenate([behind2, behind1, kv], axis=3)
    span = window.shape[3]
    query_pos = first_pos + jnp.arange(tokens, dtype=jnp.int32)
    key_pos = first_pos - 2 * tokens + jnp.arange(span, dtype=jnp.int32)
    allowed = (
        (key_pos[None, :] <= query_pos[:, None])
        & (query_pos[:, None] - key_pos[None, :] < WIN)
        & (key_pos[None, :] >= 0)
    )
    query = query.reshape(kv_heads, heads // kv_heads, HD, tokens)
    scores = (
        jnp.einsum("gjdq,gdk->gjqk", query, window[0], preferred_element_type=F32)
        * score_scale
    )
    scores = jnp.where(allowed, scores, -1e30)
    highest = jnp.max(scores, axis=-1, keepdims=True)
    mass = jnp.exp(scores - highest)
    probs = (mass / jnp.sum(mass, axis=-1, keepdims=True)).astype(BF)
    out = jnp.einsum("gjqk,gdk->gjdq", probs, window[1], preferred_element_type=F32)
    out = out.astype(BF).reshape(q_w, tokens)

    both = jnp.where(k == 0, jnp.stack([oall, ocore], 2), jnp.stack([ocore, oall], 2))
    both = both.reshape(n_col, width, q_w)

    def partial(dz, dy):
        at = (zl + dz) % NZL * NY + (y + dy) % NY
        piece = lax.dynamic_index_in_dim(both, at, 0, keepdims=False)
        return jnp.dot(piece, out, preferred_element_type=F32).astype(BF)

    parts = {(dz, dy): partial(dz, dy) for dz in range(NZL) for dy in range(NY)}
    nb = width * 2 // 3 // 16 * 16
    hb, ha = nb // 2, (width - nb) // 2

    def plus(*terms):
        return sum(t.astype(F32) for t in terms).astype(BF)

    a_in = col_perm(jnp.stack([parts[1, dy][nb:] for dy in range(NY)]), dz=1)
    ba = col_perm(jnp.stack([parts[dz, 2][:hb] for dz in range(2)]), dy=1)
    bb = col_perm(jnp.stack([parts[dz, 2][hb:nb] for dz in range(2)]), dy=-1)
    a_in, ba, bb = fence(a_in, ba, bb)
    a_sum = [plus(parts[0, dy][nb:], a_in[dy]) for dy in range(NY)]
    up = jnp.stack([parts[dz, 1][:nb] for dz in range(2)])
    up = jnp.concatenate([plus(up[:, :hb], ba), up[:, hb:]], 1)
    down = jnp.stack([parts[dz, 3][:nb] for dz in range(2)])
    down = jnp.concatenate([down[:, :hb], plus(down[:, hb:], bb)], 1)
    b_up, b_down = col_perm(up, dy=1), col_perm(down, dy=-1)
    aa, ab = col_perm(a_sum[2][:ha], dy=1), col_perm(a_sum[2][ha:], dy=-1)
    b_up, b_down, aa, ab = fence(b_up, b_down, aa, ab)
    b_in = col_perm(plus(parts[1, 0][:nb], b_up[1], b_down[1]), dz=1)
    a_up = jnp.concatenate([plus(a_sum[1][:ha], aa), a_sum[1][ha:]], 0)
    a_down = jnp.concatenate([a_sum[3][:ha], plus(a_sum[3][ha:], ab)], 0)
    a_up, a_down = col_perm(a_up, dy=1), col_perm(a_down, dy=-1)
    result = jnp.concatenate(
        [
            plus(parts[0, 0][:nb], b_up[0], b_down[0], b_in),
            plus(a_sum[0], a_up, a_down),
        ],
        0,
    )
    return result.T


def solution(mesh):
    placed = (
        P("row", "col"),
        P(),
        P("row", "col"),
        P("row", "col"),
        P("row", "col"),
        P("col", "row"),
        P(),
        P(),
    )
    return jax.shard_map(
        shards, mesh=mesh, in_specs=placed, out_specs=P("row", "col"), check_vma=False
    )
```

```python
import jax
import jax.numpy as jnp
from jax import lax
from jax.experimental import pallas as pl
from jax.experimental.pallas import tpu as pltpu
from jax.sharding import PartitionSpec as P

HD = 128
WIN = 1024
BF = jnp.bfloat16
F32 = jnp.float32


epsilon = 1e-06
score_scale = 168.0 ** (-0.5)

NX, NZ, NC, NZL, NY = 4, 4, 2, 2, 4


def row_perm(v, dx=0, dz=0, dc=0):
    route = []
    for x in range(NX):
        for z in range(NZ):
            for c in range(NC):
                to = ((x + dx) % NX * NZ + (z + dz) % NZ) * NC + (c + dc) % NC
                route.append(((x * NZ + z) * NC + c, to))
    return lax.ppermute(v, "row", route)


def col_perm(v, dz=0, dy=0):
    route = []
    for z in range(NZL):
        for y in range(NY):
            route.append((z * NY + y, (z + dz) % NZL * NY + (y + dy) % NY))
    return lax.ppermute(v, "col", route)


def fence(*values):
    return lax.optimization_barrier(values)


def angles(rows, first_pos):
    half = HD // 2
    frequency = jnp.exp(
        -(jnp.arange(half, dtype=F32) * (2.0 / HD)) * jnp.log(F32(10000.0))
    )
    positions = (first_pos + jnp.arange(rows, dtype=jnp.int32)).astype(F32)
    turn = frequency[:, None] * positions[None, :]
    return jnp.cos(turn), jnp.sin(turn)


def norm_rope(values, gain, cosine, sine):
    mean_sq = jnp.mean(values * values, axis=1, keepdims=True)
    scaled = values * lax.rsqrt(mean_sq + epsilon) * gain[None, :, None]
    first, second = scaled[:, : HD // 2], scaled[:, HD // 2 :]
    return jnp.concatenate(
        [first * cosine - second * sine, second * cosine + first * sine], axis=1
    ).astype(BF)


def place(name, shape, moves, table, prior=None):
    arrays = []
    for array, _, _ in moves:
        if not any(array is other for other in arrays):
            arrays.append(array)
    which = [[array is other for other in arrays].index(True) for array, _, _ in moves]

    def body(table_ref, *refs):
        out, sems = refs[-2], refs[-1]
        copies = []
        for n, (_, source, at) in enumerate(moves):
            ref = refs[which[n]]
            copies.append(
                pltpu.make_async_copy(
                    ref if source is None else ref.at[source],
                    out.at[at(table_ref)],
                    sems.at[n],
                )
            )
        for copy in copies:
            copy.start()
        for copy in copies:
            copy.wait()

    size = 2 * sum(a.size for a in arrays)
    anywhere = pl.BlockSpec(memory_space=pl.ANY)
    operands = [table] + arrays + ([] if prior is None else [prior])
    return pl.pallas_call(
        body,
        name=name,
        out_shape=jax.ShapeDtypeStruct(shape, BF),
        in_specs=[pl.BlockSpec(memory_space=pltpu.SMEM)] + [anywhere] * (len(operands) - 1),
        out_specs=anywhere,
        scratch_shapes=[pltpu.SemaphoreType.DMA((len(moves),))],
        input_output_aliases={} if prior is None else {len(operands) - 1: 0},
        compiler_params=pltpu.CompilerParams(vmem_limit_bytes=1 << 20),
        cost_estimate=pl.CostEstimate(flops=0, bytes_accessed=2 * size, transcendentals=0),
    )(*operands)


def attend(query, kv, behind1, behind2, bias):
    heads, _, tokens = query.shape
    group = heads // kv.shape[1]
    tile = tokens // 2
    factor = score_scale * 1.4426950408889634

    def body(bias_ref, q_ref, own_ref, one_ref, two_ref, o_ref):
        blocks = (two_ref, one_ref, own_ref)
        key_at = lax.broadcasted_iota(jnp.int32, (tile, tile), 0)
        query_at = lax.broadcasted_iota(jnp.int32, (tile, tile), 1)
        for t in range(2):
            q = q_ref[0, :, t * tile : (t + 1) * tile]
            scores = []
            for n in range(t, t + 5):
                cut = pl.ds(n % 2 * tile, tile)
                keys = blocks[n // 2][0, 0, :, cut]
                s = lax.dot_general(
                    keys, q, (((0,), (0,)), ((), ())), preferred_element_type=F32
                )
                s = s * factor
                if n == t:
                    s = jnp.where(key_at > query_at, s, -1e30)
                if n == t + 4:
                    s = jnp.where(key_at <= query_at, s, -1e30)
                if n < 4:
                    s = s + bias_ref[n // 2]
                scores.append(s)
            high = scores[0].max(0, keepdims=True)
            for s in scores[1:]:
                high = jnp.maximum(high, s.max(0, keepdims=True))
            total, out = None, None
            for n, s in zip(range(t, t + 5), scores):
                mass = jnp.exp2(s - high)
                part = mass.sum(0, keepdims=True)
                values = blocks[n // 2][1, 0, :, pl.ds(n % 2 * tile, tile)]
                term = jnp.dot(values, mass.astype(BF), preferred_element_type=F32)
                total = part if total is None else total + part
                out = term if out is None else out + term
            o_ref[0, :, t * tile : (t + 1) * tile] = (out / total).astype(BF)

    kv_spec = pl.BlockSpec((2, 1, HD, tokens), lambda h: (0, h // group, 0, 0))
    head_spec = pl.BlockSpec((1, HD, tokens), lambda h: (h, 0, 0))
    pairs = heads * tokens * 5 * tile
    return pl.pallas_call(
        body,
        name="attend",
        grid=(heads,),
        out_shape=jax.ShapeDtypeStruct(query.shape, BF),
        in_specs=[pl.BlockSpec(memory_space=pltpu.SMEM), head_spec] + [kv_spec] * 3,
        out_specs=head_spec,
        cost_estimate=pl.CostEstimate(
            flops=4 * pairs * HD, bytes_accessed=8 * query.size, transcendentals=pairs
        ),
    )(bias, query, kv, behind1, behind2)


NEAR = [(0, 0), (0, -1), (0, 1), (-1, 0), (1, 0)]
MID = [(-1, -1), (-1, 1), (1, -1), (1, 1), (0, 2), (2, 0)]
LATE = [(-1, 2), (1, 2), (2, -1), (2, 1)]
LAST = [(2, 2)]
HELD = [(dx, dz, dc) for part in (NEAR, MID, LATE, LAST) for dc in (0, 1) for dx, dz in part]


def shards(inputs, norm_gain, w_query, w_key, w_value, w_out, q_gain, k_gain):
    tokens, width = inputs.shape
    rows = w_query.shape[0]
    q_w, kv_w = w_query.shape[1], w_key.shape[1]
    heads, kv_heads = q_w // HD, kv_w // HD
    n_row, n_col = NX * NZ * NC, NZL * NY
    r, c = lax.axis_index("row"), lax.axis_index("col")
    xi, zi, k = r // (NZ * NC), r // NC % NZ, r % NC
    zl, y = c // NY, c % NY
    subs = width // rows
    wh, xh = rows // 2 // 8 * 8, subs // 2

    held = jnp.stack(
        [((xi + dx) % NX * NZ + (zi + dz) % NZ) * NC + (k + dc) % NC for dx, dz, dc in HELD]
    ).astype(jnp.int32)
    order = jnp.arange(n_row, dtype=jnp.int32)
    slot = jnp.sum(jnp.where(held[None, :] == order[:, None], order[None, :], 0), axis=1)
    blocks = jnp.stack(
        [(zl + dz) % NZL * NY + (y + dy) % NY for dz in range(NZL) for dy in range(NY)]
    ).astype(jnp.int32)
    table = jnp.sum(
        jnp.where(
            (blocks[:, None] * subs + jnp.arange(subs))[:, :, None] == order, slot, 0
        ),
        axis=2,
    ).reshape(-1)
    gain = norm_gain.reshape(n_row, rows)[held].reshape(-1, 1)

    x = inputs.T.reshape(subs, rows, tokens)
    w = jnp.concatenate([w_query, w_key, w_value], axis=1)
    o = w_out.T
    none = jnp.zeros((1,), jnp.int32)

    def stack(name, pieces):
        moves, at = [], 0
        for piece in pieces:
            for part, start in piece:
                moves.append(
                    (part, None, lambda _, at=at, s=start, n=part.shape[0]: (at, pl.ds(s, n)))
                )
            at += 1
        return place(name, (at,) + w.shape, moves, none)

    def whole(v):
        return [(v, 0)]

    def pair(a, b):
        return [(a, 0), (b, wh)]

    za, zb = row_perm(w, dz=1), row_perm(w, dz=-1)
    xa, xb = row_perm(w, dx=1), row_perm(w, dx=-1)
    ya, yb = col_perm(x, dy=1), col_perm(x, dy=-1)
    w, x, o, za, zb, xa, xb, ya, yb = fence(w, x, o, za, zb, xa, xb, ya, yb)
    p = col_perm(x, dz=1)
    z2a, z2b = row_perm(za[:wh], dz=1), row_perm(zb[wh:], dz=-1)
    yfa, yfb = col_perm(ya[:xh], dy=1), col_perm(yb[xh:], dy=-1)
    xaza, xazb = row_perm(za, dx=1), row_perm(zb, dx=1)
    xbza, xbzb = row_perm(za, dx=-1), row_perm(zb, dx=-1)
    xfa, xfb = row_perm(xa[:wh], dx=1), row_perm(xb[wh:], dx=-1)
    near = stack("near", [whole(v) for v in (w, za, zb, xa, xb)])
    cnear = row_perm(near, dc=1)
    (p, z2a, z2b, yfa, yfb, xaza, xazb, xbza, xbzb, xfa, xfb, cnear, near, o) = fence(
        p, z2a, z2b, yfa, yfb, xaza, xazb, xbza, xbzb, xfa, xfb, cnear, near, o
    )
    pya, pyb = col_perm(p, dy=1), col_perm(p, dy=-1)
    a2a, b2a = row_perm(z2a, dx=1), row_perm(z2a, dx=-1)
    a2b, b2b = row_perm(z2b, dx=1), row_perm(z2b, dx=-1)
    faza, fazb = row_perm(xaza[:wh], dx=1), row_perm(xazb[:wh], dx=1)
    fbza, fbzb = row_perm(xbza[wh:], dx=-1), row_perm(xbzb[wh:], dx=-1)
    mid = stack(
        "mid",
        [whole(v) for v in (xaza, xazb, xbza, xbzb)] + [pair(z2a, z2b), pair(xfa, xfb)],
    )
    cmid = row_perm(mid, dc=1)
    oza, ozb = row_perm(o, dz=1), row_perm(o, dz=-1)
    (pya, pyb, a2a, b2a, a2b, b2b, faza, fazb, fbza, fbzb, mid, cmid, oza, ozb, o) = fence(
        pya, pyb, a2a, b2a, a2b, b2b, faza, fazb, fbza, fbzb, mid, cmid, oza, ozb, o
    )
    pfa, pfb = col_perm(pya[:xh], dy=1), col_perm(pyb[xh:], dy=-1)
    la, lb = row_perm(a2a, dx=1), row_perm(b2b, dx=-1)
    ma, mb = row_perm(a2a, dx=1, dc=1), row_perm(b2b, dx=-1, dc=1)
    oz2a, oz2b = row_perm(oza[:wh], dz=1), row_perm(ozb[wh:], dz=-1)
    late = stack(
        "late", [pair(a2a, a2b), pair(b2a, b2b), pair(faza, fbza), pair(fazb, fbzb)]
    )
    clate = row_perm(late, dc=1)

    def channels(name, pieces, prior=None):
        moves = []
        for v, block, first in pieces:
            for j in range(v.shape[0]):
                at = block * subs + first + j
                moves.append((v, j, lambda t, at=at: t[at]))
        return place(name, (n_row, rows, tokens), moves, table, prior)

    early = [(x, 0, 0), (ya, 3, 0), (yb, 1, 0), (yfa, 2, 0), (yfb, 2, xh)]
    early = early + [(p, 4, 0), (pya, 7, 0), (pyb, 5, 0)]
    full = channels("early", early)
    (pfa, pfb, la, lb, ma, mb, late, clate, oz2a, oz2b, oza, ozb, o, full) = fence(
        pfa, pfb, la, lb, ma, mb, late, clate, oz2a, oz2b, oza, ozb, o, full
    )
    full = channels("rest", [(pfa, 6, 0), (pfb, 6, xh)], full)
    full = full.reshape(n_row * rows, tokens)
    last = jnp.concatenate([la, lb, ma, mb], 0)
    held_weights = [near, cnear, mid, cmid, late, clate, last]

    floats = full.astype(F32)
    mean_sq = jnp.mean(floats * floats, axis=0, keepdims=True)
    normed = (floats * lax.rsqrt(mean_sq + epsilon) * gain).astype(BF)

    def project(start, stop):
        total, at = 0.0, 0
        for weights in held_weights:
            weights = weights.reshape(-1, q_w + 2 * kv_w)
            n = weights.shape[0]
            total = total + lax.dot_general(
                weights[:, start:stop],
                normed[at : at + n],
                (((0,), (0,)), ((), ())),
                preferred_element_type=F32,
            )
            at += n
        return total

    ozs = jnp.zeros((NZ,) + o.shape, BF)
    oz2 = jnp.concatenate([oz2a, oz2b], 0)
    for block, dz in ((o, 0), (oza, -1), (ozb, 1), (oz2, 2)):
        ozs = lax.dynamic_update_slice(ozs, block[None], ((zi + dz) % NZ, 0, 0))

    first_pos = r * tokens
    cosine, sine = angles(tokens, first_pos)
    proj = project(q_w, q_w + 2 * kv_w)
    key = norm_rope(proj[:kv_w].reshape(kv_heads, HD, tokens), k_gain, cosine, sine)
    kv = jnp.stack([key, proj[kv_w:].reshape(kv_heads, HD, tokens).astype(BF)])
    kv, ozs = fence(kv, ozs)
    behind2 = lax.ppermute(kv, "row", [(i, i + 2) for i in range(n_row - 2)])
    mate = lax.ppermute(kv, "row", [(i, i + 1) for i in range(0, n_row, 2)])
    oxa, oxb = row_perm(ozs, dx=1), row_perm(ozs, dx=-1)
    query = norm_rope(
        project(0, q_w).reshape(heads, HD, tokens), q_gain, cosine, sine
    )
    behind2, mate, oxa, oxb, query = fence(behind2, mate, oxa, oxb, query)
    passed = lax.ppermute(behind2, "row", [(i + 1, i) for i in range(0, n_row, 2)])
    oxfa, oxfb = row_perm(oxa[:2], dx=1), row_perm(oxb[2:], dx=-1)
    cz, ca, cb = row_perm(ozs, dc=1), row_perm(oxa, dc=1), row_perm(oxb, dc=1)
    cfa, cfb = row_perm(oxfa, dc=1), row_perm(oxfb, dc=1)
    behind1 = jnp.where(k == 0, passed, mate)
    bias = jnp.where(r < jnp.array([2, 1]), F32(-1e30), F32(0.0))
    out = attend(query, kv, behind1, behind2, bias).reshape(q_w, tokens)

    spots = jnp.stack([xi, (xi + 3) % NX, (xi + 1) % NX, (xi + 2) % NX, k, 1 - k])
    moves = []
    for core, pieces in ((4, (ozs, oxa, oxb, oxfa, oxfb)), (5, (cz, ca, cb, cfa, cfb))):
        for v, at, first in zip(pieces, (0, 1, 2, 3, 3), (0, 0, 0, 0, 2)):
            cut = pl.ds(first, v.shape[0])
            moves.append(
                (v, None, lambda t, at=at, cut=cut, core=core: (t[at], cut, t[core]))
            )
    both = place("outward", (NX, NZ, NC) + o.shape, moves, spots.astype(jnp.int32))
    both = both.reshape(n_col, width, q_w)

    def partial(dz, dy):
        at = (zl + dz) % NZL * NY + (y + dy) % NY
        piece = lax.dynamic_index_in_dim(both, at, 0, keepdims=False)
        return jnp.dot(piece, out, preferred_element_type=F32).astype(BF)

    parts = {(dz, dy): partial(dz, dy) for dz in range(NZL) for dy in range(NY)}
    nb = width * 2 // 3 // 16 * 16
    hb, ha = nb // 2, (width - nb) // 2

    def plus(*terms):
        return sum(t.astype(F32) for t in terms).astype(BF)

    a_in = col_perm(jnp.stack([parts[1, dy][nb:] for dy in range(NY)]), dz=1)
    ba = col_perm(jnp.stack([parts[dz, 2][:hb] for dz in range(2)]), dy=1)
    bb = col_perm(jnp.stack([parts[dz, 2][hb:nb] for dz in range(2)]), dy=-1)
    a_in, ba, bb = fence(a_in, ba, bb)
    a_sum = [plus(parts[0, dy][nb:], a_in[dy]) for dy in range(NY)]
    up = jnp.stack([parts[dz, 1][:nb] for dz in range(2)])
    up = jnp.concatenate([plus(up[:, :hb], ba), up[:, hb:]], 1)
    down = jnp.stack([parts[dz, 3][:nb] for dz in range(2)])
    down = jnp.concatenate([down[:, :hb], plus(down[:, hb:], bb)], 1)
    b_up, b_down = col_perm(up, dy=1), col_perm(down, dy=-1)
    aa, ab = col_perm(a_sum[2][:ha], dy=1), col_perm(a_sum[2][ha:], dy=-1)
    b_up, b_down, aa, ab = fence(b_up, b_down, aa, ab)
    b_in = col_perm(plus(parts[1, 0][:nb], b_up[1], b_down[1]), dz=1)
    a_up = jnp.concatenate([plus(a_sum[1][:ha], aa), a_sum[1][ha:]], 0)
    a_down = jnp.concatenate([a_sum[3][:ha], plus(a_sum[3][ha:], ab)], 0)
    a_up, a_down = col_perm(a_up, dy=1), col_perm(a_down, dy=-1)
    result = jnp.concatenate(
        [
            plus(parts[0, 0][:nb], b_up[0], b_down[0], b_in),
            plus(a_sum[0], a_up, a_down),
        ],
        0,
    )
    return result.T


def solution(mesh):
    placed = (
        P("row", "col"),
        P(),
        P("row", "col"),
        P("row", "col"),
        P("row", "col"),
        P("col", "row"),
        P(),
        P(),
    )
    return jax.shard_map(
        shards, mesh=mesh, in_specs=placed, out_specs=P("row", "col"), check_vma=False
    )
```
